32 devices in a mesh: role: 2 (over core), wide: 4 (over y, x), tp: 4 (over z).
Axes of the slice: x: 2, y: 2, z: 4, core: 2. Of those that a mesh axis runs over, the one named last changes fastest.
Arguments:
- normed: bfloat16 [2048, 4096], P('wide', ('role', 'tp')), may hold values from -0.29882812 to 0.29882812
- queries: bfloat16 [2048, 4096], P('wide', 'tp'), may hold values from -4 to 4
- keys: bfloat16 [2048, 1024], P('wide'), may hold values from -4 to 4
- values: bfloat16 [2048, 1024], P('wide'), may hold values from -6 to 6
- attn_out: bfloat16 [2048, 4096], P('wide', 'tp'), may hold values from -0.29882812 to 0.29882812
- row_logsumexp: float32 [32, 2048], P('tp'), as said below
- out_grad: bfloat16 [2048, 4096], P('wide', ('role', 'tp')), may hold values from -6 to 6
- out_weight: bfloat16 [4096, 4096], P('tp'), may hold values from -0.09375 to 0.09375
- qkv_weight: bfloat16 [4096, 6144], P(('role', 'tp')), may hold values from -0.09375 to 0.09375
- documents: int32 [2048], replicated, may hold values from 0 to 2, as said below
- tasks: int32 [4, 8, 2], replicated, may hold values from -1 to 7, as said below
Outputs:
- normed_grad: bfloat16 [2048, 4096], P('wide', ('role', 'tp'))
- out_weight_grad: bfloat16 [4096, 4096], P('tp', ('role', 'wide'))
- qkv_weight_grad: bfloat16 [4096, 6144], P(('role', 'tp'), 'wide')
The draws below stay inside these ranges and needn't reach their ends.
Inputs may be any that keep to these rules, and one draw needn't show every extreme that they name: `documents`: document numbers never fall along the tokens, and every number from 0 to 2 is used. `tasks`: row s lists in its first slots the query blocks of server s, in [s, j, 0], followed by slots holding -1 in both places; every query block from 0 to 7 stands in exactly one slot of the table; [s, j, 1] is the block holding the first token of the document of the query block's first token. row_logsumexp[h, i] is the logarithm of the sum, over the tokens j that token i may attend, of exp(scores[h, i, j]) as computed from queries and keys.
All inputs are finite; a program needn't handle non-finite values.
Results may differ from the reference program's by a relative error of at most 0.018.
Values may be sent and summed in bfloat16 or wider, within the bound.
No kernel may reach another device: no remote copies, remote signals or barrier semaphores. Data moves between devices by JAX's collectives and lax.ppermute only.
A program may use at most 128 MiB of HBM per device.

```python
import jax
import jax.numpy as jnp
from jax import lax

D = 4096
QUERY_HEADS = 32
KEY_VALUE_HEADS = 8
HEAD_SIZE = 128
DOCS = 3
QKV = 6144
QB = 256
WINDOW_TOKENS = 2048
SERVERS = 4


def layout(random_seed):
    block_count = WINDOW_TOKENS // QB
    cut_points = jax.random.permutation(jax.random.fold_in(random_seed, 11), WINDOW_TOKENS - 1)[:DOCS - 1] + 1
    positions = jnp.arange(WINDOW_TOKENS, dtype=jnp.int32)
    documents = jnp.sum((positions[:, None] >= cut_points[None, :]).astype(jnp.int32), axis=1).astype(jnp.int32)
    leading = documents[::QB]
    doc_starts = jnp.sum((documents[None, :] < leading[:, None]).astype(jnp.int32), axis=1)
    first_blocks = (doc_starts // QB).astype(jnp.int32)
    block_ids = jnp.arange(block_count, dtype=jnp.int32)
    tile_counts = block_ids - first_blocks + 1
    ranking = jnp.argsort(-(tile_counts * block_count + (block_count - 1 - block_ids)))

    def assign(number, carry):
        plan, server_load, filled = carry
        chosen = ranking[number]
        target = jnp.argmin(server_load)
        position = filled[target]
        plan = plan.at[target, position, 0].set(chosen)
        plan = plan.at[target, position, 1].set(first_blocks[chosen])
        return (plan, server_load.at[target].add(tile_counts[chosen]), filled.at[target].add(1))
    plan = jnp.full((SERVERS, block_count, 2), -1, jnp.int32)
    server_load = jnp.zeros((SERVERS,), jnp.int32)
    plan, server_load, filled = lax.fori_loop(0, block_count, assign, (plan, server_load, server_load))
    return (documents, plan)


def query_key(random_seed):
    query_noise = jax.random.normal(jax.random.fold_in(random_seed, 21), (WINDOW_TOKENS, QUERY_HEADS * HEAD_SIZE), jnp.float32)
    noise_key = jax.random.normal(jax.random.fold_in(random_seed, 22), (WINDOW_TOKENS, KEY_VALUE_HEADS * HEAD_SIZE), jnp.float32)
    return (jnp.clip(query_noise, -4.0, 4.0).astype(jnp.bfloat16), jnp.clip(noise_key, -4.0, 4.0).astype(jnp.bfloat16))


def draw_documents(key, part):
    return layout(jax.random.fold_in(key, 5))[0]


def draw_tasks(key, part):
    return layout(jax.random.fold_in(key, 5))[1]


def draw_queries(key, part):
    return query_key(jax.random.fold_in(key, 9))[0]


def draw_keys(key, part):
    return query_key(jax.random.fold_in(key, 9))[1]


def draw_row_logsumexp(key, part):
    queries, keys = query_key(jax.random.fold_in(key, 9))
    documents = layout(jax.random.fold_in(key, 5))[0]
    query_blocks = queries.astype(jnp.float32).reshape(WINDOW_TOKENS // QB, QB, QUERY_HEADS, HEAD_SIZE)
    full_keys = jnp.repeat(keys.astype(jnp.float32).reshape(WINDOW_TOKENS, KEY_VALUE_HEADS, HEAD_SIZE), QUERY_HEADS // KEY_VALUE_HEADS, axis=1)
    positions = jnp.arange(WINDOW_TOKENS, dtype=jnp.int32)

    def one_block(index):
        rows_query = query_blocks[index]
        scores = jnp.einsum('qhd,khd->hqk', rows_query, full_keys, precision=jax.lax.Precision.HIGHEST) * HEAD_SIZE ** (-0.5)
        query_pos = index * QB + jnp.arange(QB, dtype=jnp.int32)
        allowed = (documents[query_pos][:, None] == documents[None, :]) & (positions[None, :] <= query_pos[:, None])
        masked = jnp.where(allowed[None], scores, -jnp.inf)
        return jax.nn.logsumexp(masked, axis=2)
    stacked = lax.map(one_block, jnp.arange(WINDOW_TOKENS // QB, dtype=jnp.int32))
    return jnp.transpose(stacked, (1, 0, 2)).reshape(QUERY_HEADS, WINDOW_TOKENS)


def strengthened(drawn, own_key, source, target, blocks, factor):
    owner, partner = [(jnp.arange(drawn.shape[axis_at]) // (drawn.shape[axis_at] // blocks)).reshape([-1 if axis == axis_at else 1 for axis in range(drawn.ndim)]) for axis_at in (source, target)]
    chosen = jax.random.permutation(own_key, blocks)[partner]
    strong = (owner == chosen) | (owner == (partner + blocks // 2) % blocks)
    return jnp.where(strong, factor * drawn, drawn)


def level_of(key, dims, shards, least, high):
    def one(dim, parts):
        heights = jax.random.uniform(jax.random.fold_in(jax.random.fold_in(key, 6), dim), (parts,), jnp.float32, least / len(shards), high / len(shards))
        return jnp.repeat(jnp.exp(heights), dims[dim] // parts).reshape((-1,) + (1,) * (len(dims) - dim - 1))

    loudness = one(*shards[0])
    for cut in shards[1:]:
        loudness = loudness * one(*cut)
    return loudness


def gaussian(rng, dims, width, bound, cuts=(), kind=jnp.bfloat16):
    loudness = level_of(rng, dims, cuts, -0.22, 0.18) if cuts else 1.0
    values = jax.random.normal(rng, dims, jnp.float32) * width * loudness
    return jnp.minimum(jnp.maximum(values, -bound), bound).astype(kind)


def bell_draw_with(rng, extent, scale, most, cuts, heavy, kind=jnp.bfloat16):
    array = scale * jax.random.normal(rng, extent, jnp.float32)
    if cuts:
        array = array * level_of(rng, extent, cuts, -0.22, 0.18)
    return jnp.clip(strengthened(array, jax.random.fold_in(rng, 3), *heavy), -most, most).astype(kind)


def setup_inputs(seed: int = 0) -> dict:
    streams_of = jax.random.split(jax.random.key(seed), 12)
    return {
        "normed": gaussian(streams_of[0], (WINDOW_TOKENS, D), 0.05, 0.29882812, ((0, 4), (1, 8))),
        "queries": draw_queries(jax.random.fold_in(streams_of[11], 71), 0),
        "keys": draw_keys(jax.random.fold_in(streams_of[11], 71), 0),
        "values": gaussian(streams_of[3], (WINDOW_TOKENS, KEY_VALUE_HEADS * HEAD_SIZE), 1.0, 6.0, ((0, 4),)),
        "attn_out": gaussian(streams_of[4], (WINDOW_TOKENS, QUERY_HEADS * HEAD_SIZE), 0.05, 0.29882812, ((0, 4), (1, 4))),
        "row_logsumexp": draw_row_logsumexp(jax.random.fold_in(streams_of[11], 71), 0),
        "out_grad": bell_draw_with(streams_of[6], (WINDOW_TOKENS, D), 1.0, 6.0, ((0, 4), (1, 8)), (0, 1, 8, 2.0)),
        "out_weight": gaussian(streams_of[7], (QUERY_HEADS * HEAD_SIZE, D), (QUERY_HEADS * HEAD_SIZE) ** -0.5, 0.09375, ((0, 4),)),
        "qkv_weight": gaussian(streams_of[8], (D, QKV), D ** -0.5, 0.09375, ((0, 8),)),
        "documents": draw_documents(jax.random.fold_in(streams_of[11], 71), 0),
        "tasks": draw_tasks(jax.random.fold_in(streams_of[11], 71), 0),
    }


def tile_grads(block_q, block_k, queries4, grads4, keys_three, values_three, lse3, delta3, documents):
    offsets = jnp.arange(QB, dtype=jnp.int32)
    query_pos = block_q * QB + offsets
    key_pos = block_k * QB + offsets
    query_rows = lax.dynamic_slice_in_dim(queries4, block_q * QB, QB, 0)
    grad_rows = lax.dynamic_slice_in_dim(grads4, block_q * QB, QB, 0)
    key_rows = lax.dynamic_slice_in_dim(keys_three, block_k * QB, QB, 0)
    value_rows = lax.dynamic_slice_in_dim(values_three, block_k * QB, QB, 0)
    lse_rows = lax.dynamic_slice_in_dim(lse3, block_q * QB, QB, 2)
    delta_rows = lax.dynamic_slice_in_dim(delta3, block_q * QB, QB, 2)
    query_docs = lax.dynamic_slice_in_dim(documents, block_q * QB, QB, 0)
    key_docs = lax.dynamic_slice_in_dim(documents, block_k * QB, QB, 0)
    allowed = (query_docs[:, None] == key_docs[None, :]) & (key_pos[None, :] <= query_pos[:, None])
    scores = jnp.einsum('qphd,cpd->phqc', query_rows, key_rows) * HEAD_SIZE ** -0.5
    probs = jnp.exp(jnp.where(allowed, scores - lse_rows[..., None], -jnp.inf))
    probs_low = lax.optimization_barrier(probs.astype(jnp.bfloat16)).astype(jnp.float32)
    value_grad = jnp.einsum('phqc,qphd->cpd', probs_low, grad_rows)
    prob_grad = jnp.einsum('qphd,cpd->phqc', grad_rows, value_rows)
    score_grad = (probs * (prob_grad - delta_rows[..., None]) * HEAD_SIZE ** -0.5).astype(jnp.bfloat16)
    score_grad = lax.optimization_barrier(score_grad).astype(jnp.float32)
    query_grad = jnp.einsum('phqc,cpd->qphd', score_grad, key_rows)
    key_grad = jnp.einsum('phqc,qphd->cpd', score_grad, query_rows)
    return query_grad, jnp.stack([key_grad, value_grad], axis=2)


def block_sums(left, right):
    left3 = left.reshape(SERVERS, -1, left.shape[1])
    right3 = right.reshape(SERVERS, -1, right.shape[1])

    def accumulate(running, pieces):
        partial_value = jnp.dot(pieces[0].T, pieces[1], preferred_element_type=jnp.float32)
        return running + lax.optimization_barrier(partial_value.astype(jnp.bfloat16)).astype(jnp.float32), None

    summed, ignored = lax.scan(accumulate, jnp.zeros((left.shape[1], right.shape[1]), jnp.float32), (left3, right3))
    return summed.astype(jnp.bfloat16)


def reference(normed, queries, keys, values, attn_out, row_logsumexp, out_grad, out_weight, qkv_weight, documents, tasks):
    grand_total = normed.shape[0]
    block_count = grand_total // QB
    pair_count = QUERY_HEADS // 2
    attn_grad = jnp.dot(out_grad, out_weight.T, preferred_element_type=jnp.float32).astype(jnp.bfloat16)
    grads4 = attn_grad.astype(jnp.float32).reshape(grand_total, pair_count, 2, HEAD_SIZE)
    queries4 = queries.astype(jnp.float32).reshape(grand_total, pair_count, 2, HEAD_SIZE)
    outputs4 = attn_out.astype(jnp.float32).reshape(grand_total, pair_count, 2, HEAD_SIZE)
    delta3 = jnp.transpose(jnp.sum(grads4 * outputs4, axis=3), (1, 2, 0))
    keys_three = jnp.repeat(keys.astype(jnp.float32).reshape(grand_total, KEY_VALUE_HEADS, HEAD_SIZE), 2, axis=1)
    values_three = jnp.repeat(values.astype(jnp.float32).reshape(grand_total, KEY_VALUE_HEADS, HEAD_SIZE), 2, axis=1)
    lse3 = row_logsumexp.reshape(pair_count, 2, grand_total)
    slot_blocks = tasks[:, :, 0].reshape(-1)
    slot_firsts = tasks[:, :, 1].reshape(-1)
    matches = (slot_blocks[None, :] == jnp.arange(block_count, dtype=jnp.int32)[:, None]).astype(jnp.int32)
    first_blocks = jnp.sum(matches * slot_firsts[None, :], axis=1).astype(jnp.int32)

    def query_block(block_q, carry):
        query_all, pair_all = carry

        def key_block(block_k, inner):
            partial_q, pairs_acc = inner
            tile_q, tile_kv = tile_grads(block_q, block_k, queries4, grads4, keys_three, values_three, lse3, delta3, documents)
            current = lax.dynamic_slice_in_dim(pairs_acc, block_k * QB, QB, 0)
            pairs_acc = lax.dynamic_update_slice_in_dim(pairs_acc, current + tile_kv, block_k * QB, 0)
            return partial_q + tile_q, pairs_acc

        start = jnp.zeros((QB, pair_count, 2, HEAD_SIZE), jnp.float32)
        partial_q, pair_all = lax.fori_loop(first_blocks[block_q], block_q + 1, key_block, (start, pair_all))
        rounded = partial_q.reshape(QB, QUERY_HEADS * HEAD_SIZE).astype(jnp.bfloat16)
        query_all = lax.dynamic_update_slice_in_dim(query_all, rounded, block_q * QB, 0)
        return query_all, pair_all

    initial = (jnp.zeros((grand_total, QUERY_HEADS * HEAD_SIZE), jnp.bfloat16), jnp.zeros((grand_total, pair_count, 2, HEAD_SIZE), jnp.float32))
    query_grads, pair_sums = lax.fori_loop(jnp.int32(0), jnp.int32(block_count), query_block, initial)
    lower_pair = lax.optimization_barrier(pair_sums.astype(jnp.bfloat16)).astype(jnp.float32)
    grouped_queries = jnp.sum(lower_pair.reshape(grand_total, KEY_VALUE_HEADS, 2, 2, HEAD_SIZE), axis=2).astype(jnp.bfloat16)
    key_gradients = grouped_queries[:, :, 0, :].reshape(grand_total, KEY_VALUE_HEADS * HEAD_SIZE)
    value_gradients = grouped_queries[:, :, 1, :].reshape(grand_total, KEY_VALUE_HEADS * HEAD_SIZE)
    qkv_grads = jnp.concatenate([query_grads, key_gradients, value_gradients], axis=1)
    normed_grad = jnp.dot(qkv_grads, qkv_weight.T, preferred_element_type=jnp.float32).astype(jnp.bfloat16)
    return normed_grad, block_sums(attn_out, out_grad), block_sums(normed, qkv_grads)
```

```python
import jax
import jax.numpy as jnp
from jax import lax
from jax.experimental import pallas as pl
from jax.experimental.pallas import tpu as pltpu
from jax.sharding import PartitionSpec as P

D = 4096
QUERY_HEADS = 32
KEY_VALUE_HEADS = 8
HEAD_SIZE = 128


def general(
    normed,
    queries,
    keys,
    values,
    attn_out,
    row_logsumexp,
    out_grad,
    out_weight,
    qkv_weight,
    documents,
    tasks,
):
    role_pos = lax.axis_index("role")
    is_worker = role_pos == 0
    wide_count = lax.axis_size("wide")
    wide_pos = lax.axis_index("wide")
    tp_pos = lax.axis_index("tp")
    local_rows = normed.shape[0]
    row_halves = local_rows // 2
    head_count = queries.shape[1] // HEAD_SIZE
    pair_count = head_count // 2
    kv_count = max(1, head_count // 4)
    score_scale = HEAD_SIZE ** (-0.5)
    total_rows = wide_count * local_rows
    block_count = tasks.shape[1]
    full_grad = lax.all_gather(out_grad, ("role", "tp"), axis=1, tiled=True)
    grad_half = lax.dynamic_slice_in_dim(full_grad, role_pos * (D // 2), D // 2, 1)
    out_part = lax.dot_general(
        attn_out, grad_half, (((0,), (0,)), ((), ())), preferred_element_type=jnp.float32
    )

    def worker_side():
        return lax.dot_general(
            full_grad, out_weight, (((1,), (1,)), ((), ())), preferred_element_type=jnp.float32
        ).astype(jnp.bfloat16)

    def server_side():
        return queries

    first_piece = lax.cond(is_worker, worker_side, server_side)
    kv_start = tp_pos * head_count // 4 * HEAD_SIZE
    key_cols = lax.dynamic_slice_in_dim(keys, kv_start, kv_count * HEAD_SIZE, 1)
    value_cols = lax.dynamic_slice_in_dim(values, kv_start, kv_count * HEAD_SIZE, 1)
    kv_piece = jnp.where(is_worker, key_cols, value_cols)
    out_piece = lax.dynamic_slice_in_dim(
        attn_out, role_pos * pair_count * HEAD_SIZE, pair_count * HEAD_SIZE, 1
    )
    gathered = (
        lax.all_gather(first_piece, ("role", "wide"), axis=0, tiled=True),
        lax.all_gather(kv_piece, ("role", "wide"), axis=0, tiled=True),
        lax.all_gather(out_piece, ("role", "wide"), axis=0, tiled=True),
    )
    grad_all = gathered[0][:total_rows]
    query_all = gathered[0][total_rows:]
    key_all = gathered[1][:total_rows]
    value_all = gathered[1][total_rows:]
    output_all = gathered[2].reshape(2, total_rows, pair_count, HEAD_SIZE)
    delta_all = jnp.einsum(
        "irpd,ripd->rpi",
        grad_all.reshape(total_rows, 2, pair_count, HEAD_SIZE),
        output_all,
        preferred_element_type=jnp.float32,
    ).reshape(pair_count, 2, total_rows)
    lse_all = row_logsumexp.reshape(pair_count, 2, total_rows)

    def tile(block_q, block_k, query_grad, kv_acc):
        offsets = jnp.arange(row_halves, dtype=jnp.int32)
        query_pos = block_q * row_halves + offsets
        key_pos = block_k * row_halves + offsets
        query_rows = lax.dynamic_slice_in_dim(
            query_all, block_q * row_halves, row_halves, 0
        ).reshape(row_halves, pair_count, 2, HEAD_SIZE)
        grad_rows = lax.dynamic_slice_in_dim(grad_all, block_q * row_halves, row_halves, 0).reshape(
            row_halves, pair_count, 2, HEAD_SIZE
        )
        key_rows = lax.dynamic_slice_in_dim(key_all, block_k * row_halves, row_halves, 0).reshape(
            row_halves, kv_count, HEAD_SIZE
        )
        value_rows = lax.dynamic_slice_in_dim(
            value_all, block_k * row_halves, row_halves, 0
        ).reshape(row_halves, kv_count, HEAD_SIZE)
        if head_count >= 4:
            key_rows = jnp.repeat(key_rows, 2, axis=1)
            value_rows = jnp.repeat(value_rows, 2, axis=1)
        lse_rows = lax.dynamic_slice_in_dim(lse_all, block_q * row_halves, row_halves, 2)
        delta_rows = lax.dynamic_slice_in_dim(delta_all, block_q * row_halves, row_halves, 2)
        query_docs = lax.dynamic_slice_in_dim(documents, block_q * row_halves, row_halves, 0)
        key_docs = lax.dynamic_slice_in_dim(documents, block_k * row_halves, row_halves, 0)
        allowed = (query_docs[:, None] == key_docs[None, :]) & (
            key_pos[None, :] <= query_pos[:, None]
        )
        scores = (
            jnp.einsum("qphd,cpd->phqc", query_rows, key_rows, preferred_element_type=jnp.float32)
            * score_scale
        )
        probs = jnp.exp(jnp.where(allowed, scores - lse_rows[..., None], -jnp.inf))
        probs_low = probs.astype(jnp.bfloat16)
        value_grad = jnp.einsum(
            "phqc,qphd->cpd", probs_low, grad_rows, preferred_element_type=jnp.float32
        )
        prob_grad = jnp.einsum(
            "qphd,cpd->phqc", grad_rows, value_rows, preferred_element_type=jnp.float32
        )
        score_grad = (probs * (prob_grad - delta_rows[..., None]) * score_scale).astype(
            jnp.bfloat16
        )
        query_tile = jnp.einsum(
            "phqc,cpd->qphd", score_grad, key_rows, preferred_element_type=jnp.float32
        )
        query_grad = query_grad + query_tile.reshape(row_halves, head_count * HEAD_SIZE)
        key_grad = jnp.einsum(
            "phqc,qphd->cpd", score_grad, query_rows, preferred_element_type=jnp.float32
        )
        tile_kv = jnp.concatenate([key_grad, value_grad], axis=2).reshape(
            row_halves, pair_count * 2 * HEAD_SIZE
        )
        target = block_k % 2 * wide_count + block_k // 2
        current = lax.dynamic_index_in_dim(kv_acc, target, 0, keepdims=False)
        kv_acc = lax.dynamic_update_index_in_dim(kv_acc, current + tile_kv, target, 0)
        return (query_grad, kv_acc)

    def empty_side():
        return (
            jnp.zeros((block_count, row_halves, head_count * HEAD_SIZE), jnp.float32),
            jnp.zeros((block_count, row_halves, pair_count * 2 * HEAD_SIZE), jnp.float32),
        )

    def attend_side():
        own_row = lax.dynamic_index_in_dim(tasks, wide_pos, 0, keepdims=False)

        def slot_turn(number, carry):
            query_acc, kv_acc = carry
            block_q = own_row[number, 0]
            valid = block_q >= 0
            safe_q = jnp.maximum(block_q, 0)
            upper = jnp.where(valid, safe_q + 1, 0)
            lower = jnp.where(valid, own_row[number, 1], 0)

            def key_turn(block_k, inner):
                return tile(safe_q, block_k, inner[0], inner[1])

            start = jnp.zeros((row_halves, head_count * HEAD_SIZE), jnp.float32)
            query_grad, kv_acc = lax.fori_loop(lower, upper, key_turn, (start, kv_acc))
            target = safe_q % 2 * wide_count + safe_q // 2
            current = lax.dynamic_index_in_dim(query_acc, target, 0, keepdims=False)
            query_acc = lax.dynamic_update_index_in_dim(query_acc, current + query_grad, target, 0)
            return (query_acc, kv_acc)

        return lax.fori_loop(0, block_count, slot_turn, empty_side())

    query_acc, kv_acc = lax.cond(is_worker, empty_side, attend_side)
    kv_flat = kv_acc.reshape(block_count * row_halves, pair_count * 2 * HEAD_SIZE)
    kv_sum = lax.psum_scatter(
        kv_flat.astype(jnp.bfloat16), ("role", "wide"), scatter_dimension=0, tiled=True
    )
    arrived = lax.all_to_all(
        query_acc.astype(jnp.bfloat16), ("role", "wide"), split_axis=0, concat_axis=0, tiled=True
    )
    query_piece = jnp.sum(arrived.astype(jnp.float32), axis=0).astype(jnp.bfloat16)
    head_q, key_value_head = (
        lax.all_gather(query_piece, ("role", "tp"), axis=1, tiled=True),
        lax.all_gather(kv_sum, ("role", "tp"), axis=1, tiled=True),
    )
    query_grads = head_q.reshape(row_halves, 2, QUERY_HEADS * HEAD_SIZE)
    grouped_queries = jnp.sum(
        key_value_head.reshape(row_halves, 2, KEY_VALUE_HEADS, 2, 2 * HEAD_SIZE).astype(
            jnp.float32
        ),
        axis=3,
    ).astype(jnp.bfloat16)
    key_gradients = grouped_queries[..., :HEAD_SIZE].reshape(
        row_halves, 2, KEY_VALUE_HEADS * HEAD_SIZE
    )
    value_gradients = grouped_queries[..., HEAD_SIZE:].reshape(
        row_halves, 2, KEY_VALUE_HEADS * HEAD_SIZE
    )
    qkv_grads = jnp.concatenate([query_grads, key_gradients, value_gradients], axis=2)
    normed_grad = jnp.einsum(
        "irc,nc->rin", qkv_grads, qkv_weight, preferred_element_type=jnp.float32
    )
    normed_grad = normed_grad.reshape(local_rows, qkv_weight.shape[0]).astype(jnp.bfloat16)
    qkv_part = jnp.einsum(
        "rin,irc->nc",
        normed.reshape(2, row_halves, normed.shape[1]),
        qkv_grads,
        preferred_element_type=jnp.float32,
    )
    out_sum, qkv_sum = (
        lax.psum_scatter(
            out_part.astype(jnp.bfloat16), "wide", scatter_dimension=1, tiled=True
        ).astype(jnp.float32),
        lax.psum_scatter(
            qkv_part.astype(jnp.bfloat16), "wide", scatter_dimension=1, tiled=True
        ).astype(jnp.float32),
    )
    return (normed_grad, out_sum.astype(jnp.bfloat16), qkv_sum.astype(jnp.bfloat16))


BLOCK = 256


def shift(x, move):
    roles, wides, tps = (lax.axis_size(name) for name in ("role", "wide", "tp"))
    pairs = []
    for r in range(roles):
        for w in range(wides):
            for t in range(tps):
                to = move(r, w, t)
                if to is not None:
                    pairs.append(
                        ((r * wides + w) * tps + t, (to[0] * wides + to[1]) * tps + to[2])
                    )
    return lax.ppermute(x, ("role", "wide", "tp"), pairs)


def to_role(x):
    return shift(x, lambda r, w, t: (1 - r, w, t))


def to_wide(x, k):
    return shift(x, lambda r, w, t: (r, w ^ k, t))


def columns(x, start, size):
    return lax.dynamic_slice_in_dim(x, start, size, 1)


def contract(a, b, dims):
    return lax.dot_general(a, b, (dims, ((), ())), preferred_element_type=jnp.float32)


def attention_kernel(
    where_ref, ends_ref, lse_ref, start_ref, *refs
):
    places = (len(refs) - 8) // 4
    groups = [refs[i * places : (i + 1) * places] for i in range(4)]
    qkv_refs, grad_refs, own_refs, out_refs = groups
    q_s, k_s, v_s, g_s = refs[4 * places : 4 * places + 4]
    delta_s, dq_s, dk_s, dv_s = refs[4 * places + 4 :]
    wide_pos = where_ref[0]
    length = qkv_refs[0].shape[0]
    per_place = length // BLOCK
    blocks = places * per_place
    scale = HEAD_SIZE ** (-0.5)
    ones = jnp.ones((8, HEAD_SIZE), jnp.float32)
    for place in range(places):
        token_place = jnp.bitwise_xor(wide_pos, place)
        rows = pl.ds(pl.multiple_of(token_place * length, length), length)
        q_s[rows, :] = qkv_refs[place][:, :HEAD_SIZE]
        k_s[rows, :] = qkv_refs[place][:, HEAD_SIZE : 2 * HEAD_SIZE]
        v_s[rows, :] = qkv_refs[place][:, 2 * HEAD_SIZE :]
        grads = grad_refs[place][...]
        g_s[rows, :] = grads
        products = grads.astype(jnp.float32) * own_refs[place][...].astype(jnp.float32)
        for piece in range(per_place):
            delta_s[token_place * per_place + piece] = lax.dot_general(
                ones,
                products[piece * BLOCK : (piece + 1) * BLOCK],
                (((1,), (1,)), ((), ())),
                precision=lax.Precision.HIGHEST,
                preferred_element_type=jnp.float32,
            )
    dq_s[...] = jnp.zeros_like(dq_s)
    dk_s[...] = jnp.zeros_like(dk_s)
    dv_s[...] = jnp.zeros_like(dv_s)
    key_offsets = lax.broadcasted_iota(jnp.int32, (BLOCK, BLOCK), 0)
    query_offsets = lax.broadcasted_iota(jnp.int32, (BLOCK, BLOCK), 1)

    def key_step(block_k, nothing):
        key_rows = pl.ds(pl.multiple_of(block_k * BLOCK, BLOCK), BLOCK)
        key_pos = key_offsets + block_k * BLOCK

        def query_step(block_q, nothing):
            query_rows = pl.ds(pl.multiple_of(block_q * BLOCK, BLOCK), BLOCK)
            queries = q_s[query_rows, :]
            grads = g_s[query_rows, :]
            keys = k_s[key_rows, :]
            scores = contract(keys, queries, ((1,), (1,)))
            allowed = (key_pos <= query_offsets + block_q * BLOCK) & (
                key_pos >= start_ref[block_q]
            )
            probs = jnp.where(allowed, jnp.exp(scores * scale - lse_ref[block_q]), 0.0)
            prob_grad = contract(v_s[key_rows, :], grads, ((1,), (1,)))
            score_grad = (probs * (prob_grad - delta_s[block_q][:1]) * scale).astype(jnp.bfloat16)
            dv_s[key_rows, :] += contract(probs.astype(jnp.bfloat16), grads, ((1,), (0,)))
            dk_s[key_rows, :] += contract(score_grad, queries, ((1,), (0,)))
            dq_s[query_rows, :] += contract(score_grad, keys, ((0,), (0,)))
            return nothing

        return lax.fori_loop(block_k, ends_ref[block_k], query_step, nothing)

    lax.fori_loop(0, blocks, key_step, 0)
    for place in range(places):
        token_place = jnp.bitwise_xor(wide_pos, place)
        rows = pl.ds(pl.multiple_of(token_place * length, length), length)
        out_refs[place][:, :HEAD_SIZE] = dq_s[rows, :].astype(jnp.bfloat16)
        out_refs[place][:, HEAD_SIZE : 2 * HEAD_SIZE] = dk_s[rows, :].astype(jnp.bfloat16)
        out_refs[place][:, 2 * HEAD_SIZE :] = dv_s[rows, :].astype(jnp.bfloat16)


def attention(wide_pos, ends, lse, start, qkv, grads, outs):
    places = len(qkv)
    length = qkv[0].shape[0]
    total = places * length
    vmem = pl.BlockSpec(memory_space=pltpu.VMEM)
    smem = pl.BlockSpec(memory_space=pltpu.SMEM)
    return pl.pallas_call(
        attention_kernel,
        in_specs=[smem, smem] + [vmem] * (2 + 3 * places),
        out_specs=[vmem] * places,
        out_shape=[jax.ShapeDtypeStruct((length, 3 * HEAD_SIZE), jnp.bfloat16)] * places,
        scratch_shapes=[pltpu.VMEM((total, HEAD_SIZE), jnp.bfloat16)] * 4
        + [pltpu.VMEM((total // BLOCK, 8, BLOCK), jnp.float32)]
        + [pltpu.VMEM((total, HEAD_SIZE), jnp.float32)] * 3,
        compiler_params=pltpu.CompilerParams(vmem_limit_bytes=40 * 2**20),
        name="attention",
    )(wide_pos, ends, lse, start, *qkv, *grads, *outs)


def fast(
    normed,
    queries,
    keys,
    values,
    attn_out,
    row_logsumexp,
    out_grad,
    out_weight,
    qkv_weight,
    documents,
    tasks,
):
    r, w, t = (lax.axis_index(name) for name in ("role", "wide", "tp"))
    roles, wides, tps = (lax.axis_size(name) for name in ("role", "wide", "tp"))
    rows = normed.shape[0]
    half = rows // roles
    width = qkv_weight.shape[0]
    total = wides * rows
    heads_cols = wides * HEAD_SIZE
    q_cols = QUERY_HEADS * HEAD_SIZE
    kv_cols = KEY_VALUE_HEADS * HEAD_SIZE
    places = range(wides)
    turns = range(tps)
    kv_start = (t * roles + r) * HEAD_SIZE

    grad_slots = [out_grad] + [
        shift(out_grad, lambda r, w, t, k=k: (r, w, (t + k) % tps)) for k in turns[1:]
    ]
    key_value = [columns(keys, kv_start, HEAD_SIZE), columns(values, kv_start, HEAD_SIZE)]
    qkv = []
    for k in places:
        head = r * wides + (w ^ k)
        piece = jnp.concatenate([columns(queries, head * HEAD_SIZE, HEAD_SIZE)] + key_value, 1)
        qkv.append(to_wide(piece, k) if k else piece)
    outs_half = columns(attn_out, r * heads_cols, heads_cols)
    outs = [outs_half] + [to_wide(outs_half, k) for k in places[1:]]

    sums = []
    for side in (1 - r, r):
        summed = 0.0
        for k in turns:
            weight = lax.dynamic_slice(
                out_weight,
                (side * heads_cols, (r * tps + (t - k) % tps) * width),
                (heads_cols, width),
            )
            summed = summed + contract(grad_slots[k], weight, ((1,), (1,)))
        sums.append(summed)
    other = to_role(sums[0].astype(jnp.bfloat16))
    attn_grad = (sums[1] + other.astype(jnp.float32)).astype(jnp.bfloat16)
    grads = []
    for k in places:
        piece = columns(attn_grad, (w ^ k) * HEAD_SIZE, HEAD_SIZE)
        grads.append(to_wide(piece, k) if k else piece)

    start = jnp.sum((documents[None, :] < documents[:, None]).astype(jnp.int32), axis=1)
    blocks = total // BLOCK
    last = jnp.arange(blocks, dtype=jnp.int32) * BLOCK + (BLOCK - 1)
    ends = jnp.sum((start[None, ::BLOCK] <= last[:, None]).astype(jnp.int32), axis=1)
    head = r * wides + w
    lse = lax.dynamic_slice_in_dim(row_logsumexp, head, 1, 0).reshape(blocks, 1, BLOCK)
    head_outs = [columns(x, w * HEAD_SIZE, HEAD_SIZE) for x in outs]
    pieces = attention(
        jnp.reshape(w, (1,)).astype(jnp.int32),
        ends,
        lse,
        start.reshape(blocks, 1, BLOCK),
        qkv,
        grads,
        head_outs,
    )
    arrived = [pieces[0]] + [to_wide(pieces[k], k) for k in places[1:]]

    ordered = [x[:, :HEAD_SIZE] for x in arrived]
    for bit in (1, 2):
        flip = (w & bit) != 0
        ordered = [jnp.where(flip, ordered[k ^ bit], ordered[k]) for k in places]
    key_value_grad = sum(x[:, HEAD_SIZE:].astype(jnp.float32) for x in arrived)
    unit = jnp.concatenate(ordered + [key_value_grad.astype(jnp.bfloat16)], axis=1)
    slots = [unit] + [
        shift(unit, lambda r, w, t, k=k: (r, w, (t + k) % tps)) for k in turns[1:]
    ]
    qkv_grads = jnp.zeros((rows, q_cols + 2 * kv_cols), jnp.bfloat16)
    for k in turns:
        for side, slot in ((r, slots[k]), (1 - r, to_role(slots[k]))):
            group = ((t - k) % tps) * roles + side
            for begin, start_col, size in (
                (group * heads_cols, 0, heads_cols),
                (q_cols + group * HEAD_SIZE, heads_cols, HEAD_SIZE),
                (q_cols + kv_cols + group * HEAD_SIZE, heads_cols + HEAD_SIZE, HEAD_SIZE),
            ):
                qkv_grads = lax.dynamic_update_slice_in_dim(
                    qkv_grads, slot[:, start_col : start_col + size], begin, 1
                )
    normed_grad = contract(qkv_grads, qkv_weight, ((1,), (1,))).astype(jnp.bfloat16)

    normed_places = [normed] + [to_wide(normed, k) for k in places[1:]]
    cols = (q_cols + 2 * kv_cols) // wides
    qkv_sum = contract(normed, columns(qkv_grads, w * cols, cols), ((0,), (0,)))
    mine = lax.dynamic_slice_in_dim(qkv_grads, r * half, half, 0)
    for k in places[1:]:
        got = to_wide(columns(mine, (w ^ k) * cols, cols), k)
        for side, piece in ((r, got), (1 - r, to_role(got))):
            part = lax.dynamic_slice_in_dim(normed_places[k], side * half, half, 0)
            qkv_sum = qkv_sum + contract(part, piece, ((0,), (0,)))

    stacked = jnp.stack([grad_slots[k] for k in turns])
    out_sums = [0.0, 0.0]
    for k in places:
        piece = lax.dynamic_index_in_dim(stacked, (t - (w ^ k)) % tps, 0, keepdims=False)
        piece = to_wide(piece, k) if k else piece
        for n, part in enumerate((outs[k], to_role(outs[k]))):
            out_sums[n] = out_sums[n] + contract(part, piece, ((0,), (0,)))
    first = r == 0
    out_sum = jnp.concatenate(
        [jnp.where(first, out_sums[0], out_sums[1]), jnp.where(first, out_sums[1], out_sums[0])]
    )
    return (normed_grad, out_sum.astype(jnp.bfloat16), qkv_sum.astype(jnp.bfloat16))


def solution(mesh):
    axes = dict(mesh.shape)

    def local(normed, queries, keys, values, attn_out, *rest):
        one_head = queries.shape[1] // HEAD_SIZE == axes["role"] * axes["wide"]
        square = axes["role"] == 2 and axes["wide"] == 4 and axes["tp"] == 4
        side = fast if one_head and square else general
        return side(normed, queries, keys, values, attn_out, *rest)

    in_specs = (
        P("wide", ("role", "tp")),
        P("wide", "tp"),
        P("wide", None),
        P("wide", None),
        P("wide", "tp"),
        P("tp", None),
        P("wide", ("role", "tp")),
        P("tp", None),
        P(("role", "tp"), None),
        P(),
        P(),
    )
    out_specs = (P("wide", ("role", "tp")), P("tp", ("role", "wide")), P(("role", "tp"), "wide"))
    return jax.shard_map(local, mesh=mesh, in_specs=in_specs, out_specs=out_specs, check_vma=False)
```
